512 devices in a mesh: lat: 4 (over y_hi, core), lon: 128 (over x, z, y_lo).
Axes of the slice: x: 4, y: 4 (y_hi: 2, y_lo: 2; y = y_hi * 2 + y_lo), z: 16, core: 2. Of those that a mesh axis runs over, the one named last changes fastest.
Arguments:
- features: bfloat16 [128, 1024, 1024], P('lat', 'lon'), may hold values from -18 to 18
- depth_kernel: bfloat16 [7, 7, 1024], replicated, may hold values from -0.875 to 0.875
- depth_bias: float32 [1024], replicated, may hold values from -3 to 3
- norm_gain: float32 [1024], replicated, may hold values from 0.1 to 1.9
- norm_bias: float32 [1024], replicated, may hold values from -3 to 3
- up_weight: bfloat16 [1024, 4096], P('lon', 'lat'), may hold values from -0.1875 to 0.1875
- up_bias: float32 [4096], P('lat'), may hold values from -3 to 3
- down_weight: bfloat16 [1024, 4096], P('lon', 'lat'), may hold values from -0.09375 to 0.09375
- down_bias: float32 [1024], replicated, may hold values from -3 to 3
- layer_scale: float32 [1024], replicated, may hold values from 0.3 to 2
Outputs:
- updated: bfloat16 [128, 1024, 1024], P('lat', 'lon')
The draws below stay inside these ranges and needn't reach their ends.
All inputs are finite; a program needn't handle non-finite values.
Results may differ from the reference program's by a relative error of at most 0.0085.
Values may be sent and summed in bfloat16 or wider, within the bound.
A program may use at most 64 MiB of HBM per device.

```python
import math
import jax
import jax.numpy as jnp
from jax import lax

C = 1024
HID = 4096
HEIGHT = 128
WIDTH = 1024
N_LAT = 4


def draw_features(key, part):
    first, second = jax.random.split(jax.random.fold_in(key, 17), 2)
    channel_scale = jnp.exp(jax.random.uniform(second, (C,), jnp.float32, -1.2, 1.2))
    base = jax.random.truncated_normal(first, -4.0, 4.0, (HEIGHT, WIDTH, C), jnp.float32)
    values = base * channel_scale
    return values.astype(jnp.bfloat16)


def steps_of(key, dims, pieces, least, largest):
    def one(axis_at, shards_of):
        draws = jax.random.uniform(jax.random.fold_in(jax.random.fold_in(key, 6), axis_at), (shards_of,), jnp.float32, least / len(pieces), largest / len(pieces))
        return jnp.repeat(jnp.exp(draws), dims[axis_at] // shards_of).reshape((-1,) + (1,) * (len(dims) - axis_at - 1))

    loudness = one(*pieces[0])
    for cut in pieces[1:]:
        loudness = loudness * one(*cut)
    return loudness


def centred(rng, dims, scale, bound, pieces=(), dtype=jnp.bfloat16):
    level = steps_of(rng, dims, pieces, -0.22, 0.18) if pieces else 1.0
    result = jax.random.normal(rng, dims, jnp.float32) * scale * level
    return jnp.minimum(jnp.maximum(result, -bound), bound).astype(dtype)


def setup_inputs(seed: int = 0) -> dict:
    splits = jax.random.split(jax.random.key(seed), 11)
    return {
        "features": draw_features(jax.random.fold_in(splits[10], 71), 0),
        "depth_kernel": centred(splits[1], (7, 7, C), 49 ** -0.5, 0.875),
        "depth_bias": centred(splits[2], (C,), 0.5, 3.0, (), jnp.float32),
        "norm_gain": jnp.clip(1.0 + 0.18 * jax.random.normal(splits[3], (C,), jnp.float32), 0.1, 1.9),
        "norm_bias": centred(splits[4], (C,), 0.5, 3.0, (), jnp.float32),
        "up_weight": centred(splits[5], (C, HID), C ** -0.5, 0.1875, ((0, 128), (1, 4))),
        "up_bias": centred(splits[6], (HID,), 0.5, 3.0, ((0, 4),), jnp.float32),
        "down_weight": centred(splits[7], (C, HID), HID ** -0.5, 0.09375, ((0, 128), (1, 4))),
        "down_bias": centred(splits[8], (C,), 0.5, 3.0, (), jnp.float32),
        "layer_scale": jnp.clip(jnp.exp(jax.random.uniform(splits[9], (C,), jnp.float32, math.log(0.3), math.log(2.0))), 0.3, 2.0),
    }


def depthwise_conv(features, depth_kernel, depth_bias):
    values = features.astype(jnp.float32)
    wrapped = jnp.concatenate([values[:, -3:], values, values[:, :3]], axis=1)
    padded = jnp.pad(wrapped, ((3, 3), (0, 0), (0, 0)))
    height, width = (features.shape[0], features.shape[1])
    total = jnp.zeros(values.shape, jnp.float32) + depth_bias.astype(jnp.float32)
    kernel = depth_kernel.astype(jnp.float32)
    for row_off in range(7):
        for col_off in range(7):
            total = total + padded[row_off:row_off + height, col_off:col_off + width] * kernel[row_off, col_off]
    return total

def layer_norm(values, norm_gain, norm_bias):
    centre = lax.optimization_barrier(jnp.mean(values, axis=-1, keepdims=True))
    spread = lax.optimization_barrier(jnp.mean((values - centre) ** 2, axis=-1, keepdims=True))
    return ((values - centre) * lax.rsqrt(spread + 1e-06) * norm_gain + norm_bias).astype(jnp.bfloat16)

def reference(features, depth_kernel, depth_bias, norm_gain, norm_bias, up_weight, up_bias, down_weight, down_bias, layer_scale):
    depthwise = depthwise_conv(features, depth_kernel, depth_bias)
    normed = layer_norm(depthwise, norm_gain, norm_bias)
    quarter = HID // N_LAT

    def one_row(row_pixels):
        pre = jnp.dot(row_pixels, up_weight, preferred_element_type=jnp.float32) + up_bias
        hidden = jax.nn.gelu(pre, approximate=False).astype(jnp.bfloat16)
        branch = jnp.zeros((row_pixels.shape[0], C), jnp.float32)
        for block in range(N_LAT):
            part_hidden = hidden[:, block * quarter:(block + 1) * quarter]
            part_weight = down_weight[:, block * quarter:(block + 1) * quarter]
            product = lax.dot_general(part_hidden, part_weight, (((1,), (1,)), ((), ())), preferred_element_type=jnp.float32)
            rounded = lax.optimization_barrier(product.astype(jnp.bfloat16))
            branch = branch + rounded.astype(jnp.float32)
        return branch
    branch = lax.map(one_row, normed)
    updated = features.astype(jnp.float32) + layer_scale * (branch + down_bias)
    return updated.astype(jnp.bfloat16)
```

```python
import jax
import jax.numpy as jnp
from jax import lax
from jax.sharding import PartitionSpec as P


def with_halo(block, sides, width, periodic):
    for axis, dim in sides:
        count = lax.axis_size(axis)
        forward = [(i, i + 1) for i in range(count - 1)]
        if periodic:
            forward.append((count - 1, 0))
        backward = [(target, source) for source, target in forward]
        low = lax.ppermute(
            lax.slice_in_dim(block, block.shape[dim] - width, None, axis=dim), axis, forward
        )
        high = lax.ppermute(lax.slice_in_dim(block, 0, width, axis=dim), axis, backward)
        block = jnp.concatenate([low, block, high], axis=dim)
    return block


def staged_gather(shard):
    count = lax.axis_size("lon")
    n_x, n_y = 4, 2
    n_z = count // (n_x * n_y)
    index = lambda x, z, y: (x * n_z + z) * n_y + y
    by_y = [[index(x, z, y) for y in range(n_y)] for x in range(n_x) for z in range(n_z)]
    by_x = [[index(x, z, y) for x in range(n_x)] for z in range(n_z) for y in range(n_y)]
    by_z = [[index(x, z, y) for z in range(n_z)] for x in range(n_x) for y in range(n_y)]
    part = lax.all_gather(shard, "lon", axis=0, axis_index_groups=by_y)
    part = lax.all_gather(part, "lon", axis=0, axis_index_groups=by_x)
    part = lax.all_gather(part, "lon", axis=0, axis_index_groups=by_z)
    part = jnp.swapaxes(part, 0, 1)
    return part.reshape((count * shard.shape[0],) + shard.shape[1:])


def local(
    features,
    depth_kernel,
    depth_bias,
    norm_gain,
    norm_bias,
    up_weight,
    up_bias,
    down_weight,
    down_bias,
    layer_scale,
):
    row_count, col_count, chan_count = features.shape
    circled = with_halo(features, (("lon", 1),), 3, True)
    padded = with_halo(circled, (("lat", 0),), 3, False)
    kernel = depth_kernel.astype(jnp.float32)
    total = jnp.zeros((row_count, col_count, chan_count), jnp.float32) + depth_bias
    for row_off in range(7):
        for col_off in range(7):
            window = padded[row_off : row_off + row_count, col_off : col_off + col_count].astype(
                jnp.float32
            )
            total = total + window * kernel[row_off, col_off]
    centre = jnp.mean(total, axis=-1, keepdims=True)
    spread = jnp.mean((total - centre) ** 2, axis=-1, keepdims=True)
    normed = ((total - centre) * lax.rsqrt(spread + 1e-06) * norm_gain + norm_bias).astype(
        jnp.bfloat16
    )
    normed = normed.reshape(row_count * col_count, chan_count)
    gathered = lax.all_gather(normed, "lat", axis=0, tiled=True)
    pre = (
        jnp.dot(
            gathered,
            staged_gather(up_weight),
            preferred_element_type=jnp.float32,
        )
        + up_bias
    )
    hidden = jax.nn.gelu(pre, approximate=False).astype(jnp.bfloat16)
    partial_out = lax.dot_general(
        hidden,
        staged_gather(down_weight),
        (((1,), (1,)), ((), ())),
        preferred_element_type=jnp.float32,
    )
    branch = lax.psum_scatter(
        partial_out.astype(jnp.bfloat16), "lat", scatter_dimension=0, tiled=True
    ).astype(jnp.float32)
    branch = branch.reshape(row_count, col_count, chan_count)
    updated = features.astype(jnp.float32) + layer_scale * (branch + down_bias)
    return updated.astype(jnp.bfloat16)


def solution(mesh):
    placed = (
        P("lat", "lon", None),
        P(),
        P(),
        P(),
        P(),
        P("lon", "lat"),
        P("lat"),
        P("lon", "lat"),
        P(),
        P(),
    )
    return jax.shard_map(
        local, mesh=mesh, in_specs=placed, out_specs=P("lat", "lon", None), check_vma=False
    )
```

```python
import functools

import jax
import jax.numpy as jnp
from jax import lax
from jax.experimental import pallas as pl
from jax.experimental.pallas import tpu as pltpu
from jax.sharding import PartitionSpec as P

MESH = pl.DeviceIdType.MESH
NX, NZ, NY = 4, 16, 2
STEPS = NZ // 2


def remote(src, dst, send_sem, recv_sem, device):
    return pltpu.make_async_remote_copy(
        src_ref=src, dst_ref=dst, send_sem=send_sem, recv_sem=recv_sem, device_id=device, device_id_type=MESH
    )


def kernel(
    feat, dker, dbias, gain, nbias, up, ubias, down, obias, scale,
    out,
    wts, ybuf, xpad, kers, conv, csend, crecv, rrecv, acts, hid, own, s_sib, s_mid, s_crs, r_sib, r_mid, r_crs,
    y_ss, y_rs, h_ss, h_rs, x1_ss, x1_rs, x2_ss, x2_rs, z1_ss, z1_rs, z2_ss, z2_rs, a_ss, a_rs, o_ss, o_rs,
):
    f32, bf16 = jnp.float32, jnp.bfloat16
    rows, cols, chans = feat.shape
    hidden = up.shape[1]
    tiles = chans // 128
    half = hidden // 2
    blocks = rows // 8
    chunk = 8 * cols
    pixels = rows * cols
    n_lon = NX * NZ * NY
    lat = lax.axis_index("lat")
    lon = lax.axis_index("lon")
    y = lax.rem(lon, NY)
    z = lax.rem(lon // NY, NZ)
    x = lon // (NY * NZ)

    def at(x_, z_):
        return (lat, (lax.rem(x_ + NX, NX) * NZ + lax.rem(z_ + NZ, NZ)) * NY + y)

    flip = lat + 1 - 2 * lax.rem(lat, 2)
    far = lax.rem(lat + 2, 4)
    far_flip = lax.rem(flip + 2, 4)
    pair_lon = lon + 1 - 2 * y
    pair = (lat, pair_lon)
    sib = (flip, lon)
    crs = (far, pair_lon)
    east = lax.rem(lon + 1, n_lon)
    west = lax.rem(lon + n_lon - 1, n_lon)
    has_up = lat > 0
    has_down = lat < 3

    barrier = pltpu.get_barrier_semaphore()

    def hello(device):
        pl.semaphore_signal(barrier, inc=1, device_id=device, device_id_type=MESH)

    near = [pair, sib, crs, (lat, east), (lat, west), at(x, z + 1), at(x, z - 1)]
    near += [at(x + k, z) for k in range(1, NX)]
    for device in near:
        hello(device)

    @pl.when(has_up)
    def _():
        for lon_ in (west, lon, east):
            hello((lat - 1, lon_))

    @pl.when(has_down)
    def _():
        for lon_ in (west, lon, east):
            hello((lat + 1, lon_))

    for a in range(7):
        kers[a, 0:7, :] = dker[a].astype(f32)

    low4 = lax.broadcasted_iota(jnp.int32, (8, chans), 0) < 4

    def pack(q, _):
        v = [feat[4 * q + i].astype(f32) for i in range(4)]
        turned = [pltpu.roll(t, 4, 0) for t in v]
        right = [jnp.where(low4, turned[i], v[i + 1]) for i in (0, 2)]
        left = [jnp.where(low4, v[i], turned[i + 1]) for i in (0, 2)]
        csend[0, q] = jnp.concatenate(right, 0).astype(bf16)
        csend[1, q] = jnp.concatenate(left, 0).astype(bf16)
        return 0

    lax.fori_loop(0, rows // 4, pack, 0)
    pl.semaphore_wait(barrier, len(near) + 3 * has_up.astype(jnp.int32) + 3 * has_down.astype(jnp.int32))

    ycopy = [remote((up, down)[w], ybuf.at[w], y_ss.at[w], y_rs.at[w], pair) for w in range(2)]
    for c in ycopy:
        c.start()

    last = rows // 4 - 1
    to_east = remote(csend.at[0], crecv.at[0, pl.ds(1, last + 1)], h_ss.at[0], h_rs.at[0], (lat, east))
    to_west = remote(csend.at[1], crecv.at[1, pl.ds(1, last + 1)], h_ss.at[1], h_rs.at[1], (lat, west))
    to_east.start()
    to_west.start()
    to_down = [
        remote(feat.at[pl.ds(rows - 3, 3)], rrecv.at[0], h_ss.at[2], h_rs.at[2], (lat + 1, lon)),
        remote(csend.at[0, last], crecv.at[0, 0], h_ss.at[3], h_rs.at[3], (lat + 1, east)),
        remote(csend.at[1, last], crecv.at[1, 0], h_ss.at[4], h_rs.at[4], (lat + 1, west)),
    ]
    to_up = [
        remote(feat.at[pl.ds(0, 3)], rrecv.at[1], h_ss.at[5], h_rs.at[5], (lat - 1, lon)),
        remote(csend.at[0, 0], crecv.at[0, last + 2], h_ss.at[6], h_rs.at[6], (lat - 1, east)),
        remote(csend.at[1, 0], crecv.at[1, last + 2], h_ss.at[7], h_rs.at[7], (lat - 1, west)),
    ]

    @pl.when(has_down)
    def _():
        for c in to_down:
            c.start()

    @pl.when(has_up)
    def _():
        for c in to_up:
            c.start()

    def widen(h, _):
        v = feat[h].astype(f32)
        for t in range(tiles):
            xpad[t, h + 4, 8:16, :] = v[:, t * 128 : (t + 1) * 128]
        return 0

    lax.fori_loop(0, rows, widen, 0)

    prow = 2 * up.shape[0]

    def wide(w, zb):
        return wts.at[w, :, pl.ds(pl.multiple_of(zb * prow, prow), prow), pl.ds(0, half)]

    def thin(w, xb, zb):
        return wts.at[w, xb, pl.ds(pl.multiple_of(zb * prow, prow), prow), pl.ds(half, half)]

    def first(w, xb, zb):
        return wts.at[w, xb, pl.ds(pl.multiple_of(zb * prow, prow), prow), pl.ds(0, half)]

    def length(w, d):
        return STEPS if w == d else STEPS - 1

    def block(d, s):
        return lax.rem(z + (NZ - s if d == 0 else s), NZ)

    def z1(w, d, s):
        ref = wide(w, block(d, s))
        return remote(ref, ref, z1_ss.at[w, d, s], z1_rs.at[w, d, s], at(x, z + 1 if d == 0 else z - 1))

    def z2(w, d, s):
        ref = thin(w, x, block(d, s))
        return remote(ref, ref, z2_ss.at[w, d, s], z2_rs.at[w, d, s], at(x, z + 1 if d == 0 else z - 1))

    def x1(w, k):
        ref = first(w, x, z)
        return remote(ref, ref, x1_ss.at[w, k - 1], x1_rs.at[w, k - 1], at(x + k, z))

    def x2(w, k, zb):
        ref = thin(w, x, zb)
        return remote(ref, ref, x2_ss.at[w, k - 1], x2_rs.at[w, k - 1], at(x + k, z))

    for w in range(2):
        ycopy[w].wait_recv()
        mine = (up, down)[w][...].astype(f32)
        other = ybuf[w].astype(f32)
        is_low = y == 0
        both = jnp.concatenate([jnp.where(is_low, mine, other), jnp.where(is_low, other, mine)], 0)
        wts[w, x, pl.ds(pl.multiple_of(z * prow, prow), prow), :] = both.astype(bf16)
        for k in range(1, NX):
            x1(w, k).start()
        for d in range(2):
            z2(w, d, 0).start()
        for k in range(1, NX):
            x2(w, k, z).start()

    def serve(w, s, final=False):
        for d in range(2):
            z2(w, d, s).wait_recv()
            if not final:
                z2(w, d, s + 1).start()
            for k in range(1, NX):
                x2(w, k, block(d, s + 1)).start()
        for d in range(2):
            z1(w, d, s).wait_recv()
            if not final:
                z1(w, d, s + 1).start()

    def serve_end(w):
        s = STEPS - 2
        long, short = w, 1 - w
        z2(w, long, s).wait_recv()
        z2(w, long, s + 1).start()
        for k in range(1, NX):
            x2(w, k, block(long, s + 1)).start()
        z1(w, long, s).wait_recv()
        z1(w, long, s + 1).start()
        z2(w, short, s).wait_recv()
        for k in range(1, NX):
            x2(w, k, block(short, s + 1)).start()
        z1(w, short, s).wait_recv()

    def serve_last(w):
        s = STEPS - 1
        z2(w, w, s).wait_recv()
        for k in range(1, NX):
            x2(w, k, block(w, s + 1)).start()
        z1(w, w, s).wait_recv()

    def whole(w, k):
        ref = wts.at[w, 0, :, pl.ds(0, half)]
        return remote(ref, ref, x2_ss.at[w, k - 1], x2_rs.at[w, k - 1], at(x + k, z))

    for w in range(2):
        for k in range(1, NX):
            x1(w, k).wait_recv()
        for d in range(2):
            z1(w, d, 0).start()

    to_east.wait_recv()
    to_west.wait_recv()

    def place(q):
        for side, lo in ((0, 4), (1, 16)):
            v = crecv[side, q].astype(f32)
            for i in range(4):
                for t in range(tiles):
                    xpad[t, 4 * q + i, lo : lo + 4, :] = v[4 * i : 4 * i + 4, t * 128 : (t + 1) * 128]

    def place_loop(q, _):
        place(q)
        return 0

    lax.fori_loop(1, last + 2, place_loop, 0)

    def margin(present, copies, row0, q, slot):
        @pl.when(present)
        def _():
            for c in copies:
                c.wait_recv()
            place(q)
            for r in range(3):
                v = rrecv[slot, r].astype(f32)
                for t in range(tiles):
                    xpad[t, row0 + r, 8:16, :] = v[:, t * 128 : (t + 1) * 128]

        @pl.when(jnp.logical_not(present))
        def _():
            for r in range(3):
                for t in range(tiles):
                    xpad[t, row0 + r] = jnp.zeros((24, 128), f32)

    margin(has_up, to_down, 1, 0, 0)
    margin(has_down, to_up, rows + 4, last + 2, 1)

    def conv_tile(rb, t):
        lanes = pl.ds(pl.multiple_of(t * 128, 128), 128)
        acc = [jnp.broadcast_to(dbias[:, lanes], (8, 128)) for _ in range(8)]
        for b in range(7):
            win = [xpad[t, rb * 8 + 1 + r, 5 + b : 13 + b, :] for r in range(14)]
            for a in range(7):
                k = jnp.broadcast_to(kers[a, b : b + 1, lanes], (8, 128))
                for o in range(8):
                    acc[o] = acc[o] + win[o + a] * k
        for o in range(8):
            conv[pl.ds(pl.multiple_of((rb * 8 + o) * 8, 8), 8), lanes] = acc[o]

    def norm_group(rb, g):
        px = pl.ds(pl.multiple_of(rb * chunk + g * 16, 16), 16)
        v = conv[px, :]
        v = v - jnp.mean(v, axis=-1, keepdims=True)
        var = jnp.mean(v * v, axis=-1, keepdims=True)
        v = v * lax.rsqrt(var + 1e-06) * gain[...] + nbias[...]
        acts[lat, px, :] = v.astype(bf16)

    def act(slot, c):
        return acts.at[slot, pl.ds(pl.multiple_of(c * chunk, chunk), chunk), :]

    def a_sib(c):
        return remote(act(lat, c), act(lat, c), a_ss.at[0, c], a_rs.at[0, c], sib)

    def a_crs(c):
        return remote(act(lat, c), act(lat, c), a_ss.at[1, c], a_rs.at[1, c], crs)

    def a_fwd(c):
        return remote(act(far, c), act(far, c), a_ss.at[2, c], a_rs.at[2, c], sib)

    def conv_block(rb, _):
        def run(t, _):
            conv_tile(rb, t)
            return 0

        lax.fori_loop(0, tiles // 2, run, 0)
        serve(0, rb)
        lax.fori_loop(tiles // 2, tiles, run, 0)

        def run_norm(g, _):
            norm_group(rb, g)
            return 0

        lax.fori_loop(0, chunk // 16, run_norm, 0)
        a_crs(rb).start()
        a_sib(rb).start()
        serve(1, rb)
        return 0

    lax.fori_loop(0, blocks, conv_block, 0)

    def forward(c):
        a_crs(c).wait_recv()
        a_fwd(c).start()

    pending = list(range(blocks))
    for s in range(blocks, STEPS):
        for w in range(2):
            if s < STEPS - 2:
                serve(w, s)
            elif s == STEPS - 2:
                serve_end(w)
            else:
                serve_last(w)
            if w == 0 and pending:
                forward(pending.pop(0))
    for c in pending:
        forward(c)

    for k in range(1, NX):
        whole(0, k).wait_recv()

    def pointwise(q):
        def one(n, _):
            lanes = pl.ds(pl.multiple_of(n * 256, 256), 256)
            wt = wts[0, :, :, lanes].reshape(chans, 256)
            pre = jnp.dot(acts[q], wt, preferred_element_type=f32) + ubias[:, lanes]
            act_ = 0.5 * pre * (1.0 + lax.erf(pre * 0.7071067811865476))
            hid[:, lanes] = act_.astype(bf16)
            return 0

        lax.fori_loop(0, hidden // 256, one, 0)

    def project(n):
        return lax.dot_general(hid[...], wts[1, n], (((1,), (1,)), ((), ())), preferred_element_type=f32)

    def o_copy(kind, n):
        src, dst, device = ((s_sib, r_sib, sib), (s_mid, r_mid, crs), (s_crs, r_crs, sib))[kind]
        return remote(src.at[n], dst.at[n], o_ss.at[kind, n], o_rs.at[kind, n], device)

    parts = NX
    for c in range(blocks):
        a_sib(c).wait_recv()
        a_fwd(c).wait_recv()

    pointwise(far_flip)
    for k in range(1, NX):
        whole(1, k).wait_recv()

    def first_part(n, _):
        s_sib[n] = project(n).astype(bf16)
        o_copy(0, n).start()
        return 0

    lax.fori_loop(0, parts, first_part, 0)

    pointwise(far)

    def second_part(n, _):
        total = project(n)
        o_copy(0, n).wait_recv()
        s_mid[n] = (total + r_sib[n].astype(f32)).astype(bf16)
        o_copy(1, n).start()
        return 0

    lax.fori_loop(0, parts, second_part, 0)

    pointwise(flip)

    def third_part(n, _):
        s_crs[n] = project(n).astype(bf16)
        o_copy(2, n).start()
        return 0

    lax.fori_loop(0, parts, third_part, 0)

    pointwise(lat)

    def own_part(n, _):
        own[n] = project(n)
        return 0

    lax.fori_loop(0, parts, own_part, 0)

    def finish(n, _):
        width = chans // parts
        lanes = pl.ds(pl.multiple_of(n * width, width), width)
        o_copy(2, n).wait_recv()
        part = own[n] + r_crs[n].astype(f32)
        o_copy(1, n).wait_recv()
        part = part + r_mid[n].astype(f32)
        part = scale[:, lanes] * (part + obias[:, lanes])
        res = feat[:, :, lanes].astype(f32) + part.reshape(rows, cols, width)
        out[:, :, lanes] = res.astype(bf16)
        return 0

    lax.fori_loop(0, parts, finish, 0)

    for w in range(2):
        ycopy[w].wait_send()
        for k in range(1, NX):
            x1(w, k).wait_send()
            whole(w, k).wait_send()
        for d in range(2):

            def gone(s, _, w=w, d=d):
                z1(w, d, s).wait_send()
                z2(w, d, s).wait_send()
                return 0

            lax.fori_loop(0, length(w, d), gone, 0)
    to_east.wait_send()
    to_west.wait_send()

    @pl.when(has_down)
    def _():
        for c in to_down:
            c.wait_send()

    @pl.when(has_up)
    def _():
        for c in to_up:
            c.wait_send()

    for c in range(blocks):
        a_sib(c).wait_send()
        a_crs(c).wait_send()
        a_fwd(c).wait_send()
    for n in range(parts):
        for kind in range(3):
            o_copy(kind, n).wait_send()


def local(
    features, depth_kernel, depth_bias, norm_gain, norm_bias, up_weight, up_bias, down_weight, down_bias, layer_scale
):
    rows, cols, chans = features.shape
    shard, hidden = up_weight.shape
    pixels = rows * cols
    bf16, f32 = jnp.bfloat16, jnp.float32
    vmem, dma = pltpu.VMEM, pltpu.SemaphoreType.DMA
    blocks = rows // 8
    flat = lambda v: v.reshape(1, -1)
    spec = pl.BlockSpec(memory_space=pltpu.VMEM)
    piece = (NX, pixels, chans // NX)
    return pl.pallas_call(
        kernel,
        out_shape=jax.ShapeDtypeStruct(features.shape, features.dtype),
        in_specs=[spec] * 10,
        out_specs=spec,
        scratch_shapes=[
            vmem((2, NX, chans // NX, hidden), bf16),
            vmem((2, shard, hidden), bf16),
            vmem((chans // 128, rows + 8, 24, 128), f32),
            vmem((7, 8, chans), f32),
            vmem((pixels, chans), f32),
            vmem((2, rows // 4, 16, chans), bf16),
            vmem((2, rows // 4 + 2, 16, chans), bf16),
            vmem((2, 3, cols, chans), bf16),
            vmem((4, pixels, chans), bf16),
            vmem((pixels, hidden), bf16),
            vmem(piece, f32),
            vmem(piece, bf16),
            vmem(piece, bf16),
            vmem(piece, bf16),
            vmem(piece, bf16),
            vmem(piece, bf16),
            vmem(piece, bf16),
            dma((2,)), dma((2,)),
            dma((8,)), dma((8,)),
            dma((2, NX - 1)), dma((2, NX - 1)),
            dma((2, NX - 1)), dma((2, NX - 1)),
            dma((2, 2, STEPS)), dma((2, 2, STEPS)),
            dma((2, 2, STEPS)), dma((2, 2, STEPS)),
            dma((3, blocks)), dma((3, blocks)),
            dma((3, NX)), dma((3, NX)),
        ],
        compiler_params=pltpu.CompilerParams(
            collective_id=0, has_side_effects=True, vmem_limit_bytes=48 << 20
        ),
    )(
        features, depth_kernel, flat(depth_bias), flat(norm_gain), flat(norm_bias), up_weight, flat(up_bias),
        down_weight, flat(down_bias), flat(layer_scale),
    )


def solution(mesh):
    placed = (
        P("lat", "lon", None), P(), P(), P(), P(), P("lon", "lat"), P("lat"), P("lon", "lat"), P(), P(),
    )
    return jax.shard_map(
        local, mesh=mesh, in_specs=placed, out_specs=P("lat", "lon", None), check_vma=False
    )
```

```python
import functools

import jax
import jax.numpy as jnp
from jax import lax
from jax.experimental import pallas as pl
from jax.experimental.pallas import tpu as pltpu
from jax.sharding import PartitionSpec as P

MESH = pl.DeviceIdType.MESH
NX, NZ, NY = 4, 16, 2
STEPS = NZ // 2
EARLY = 1
DIRECT = STEPS - 2


def remote(src, dst, send_sem, recv_sem, device):
    return pltpu.make_async_remote_copy(
        src_ref=src, dst_ref=dst, send_sem=send_sem, recv_sem=recv_sem, device_id=device, device_id_type=MESH
    )


def kernel(
    feat_h, dker_h, dbias_h, gain_h, nbias_h, up, ubias_h, down, obias_h, scale_h,
    out,
    feat, dker, dbias, gain, nbias, ubias, obias, scale,
    wts, xpad, kers, conv, csend, crecv, rrecv, acts, hid, own, s_sib, s_mid, s_crs, r_sib, r_mid, r_crs,
    in_s, own_s, y_ss, y_rs, h_ss, h_rs, hc_ss, hc_rs, x1_ss, x1_rs, x2_ss, x2_rs, xf_ss, xf_rs, z1_ss, z1_rs, z2_ss, z2_rs, a_ss, a_rs, o_ss, o_rs,
):
    f32, bf16 = jnp.float32, jnp.bfloat16
    rows, cols, chans = feat.shape
    hidden = up.shape[1]
    tiles = chans // 128
    wide_l = hidden // 4
    thin_l = hidden - wide_l
    blocks = rows // 8
    chunk = 8 * cols
    pixels = rows * cols
    n_lon = NX * NZ * NY
    lat = lax.axis_index("lat")
    lon = lax.axis_index("lon")
    y = lax.rem(lon, NY)
    z = lax.rem(lon // NY, NZ)
    x = lon // (NY * NZ)

    def at(x_, z_, y_=y):
        return (lat, (lax.rem(x_ + NX, NX) * NZ + lax.rem(z_ + NZ, NZ)) * NY + y_)

    flip = lat + 1 - 2 * lax.rem(lat, 2)
    far = lax.rem(lat + 2, 4)
    far_flip = lax.rem(flip + 2, 4)
    pair_lon = lon + 1 - 2 * y
    pair = (lat, pair_lon)
    sib = (flip, lon)
    crs = (far, pair_lon)
    east = lax.rem(lon + 1, n_lon)
    west = lax.rem(lon + n_lon - 1, n_lon)
    has_up = lat > 0
    has_down = lat < 3

    barrier = pltpu.get_barrier_semaphore()

    def hello(device):
        pl.semaphore_signal(barrier, inc=1, device_id=device, device_id_type=MESH)

    near = [pair, sib, crs, (lat, east), (lat, west), at(x, z + 1), at(x, z - 1)]
    near += [at(x + k, z, y_) for k in range(1, NX) for y_ in (y, 1 - y)]
    for device in near:
        hello(device)

    @pl.when(has_up)
    def _():
        for lon_ in (west, lon, east):
            hello((lat - 1, lon_))

    @pl.when(has_down)
    def _():
        for lon_ in (west, lon, east):
            hello((lat + 1, lon_))

    shard = up.shape[0]
    mine = pl.ds(pl.multiple_of((z * NY + y) * shard, shard), shard)
    own_copy = [pltpu.make_async_copy((up, down)[w], wts.at[w, x, mine, :], own_s.at[w]) for w in range(2)]
    loads = [
        pltpu.make_async_copy(a, b, in_s.at[i])
        for i, (a, b) in enumerate(
            (
                (feat_h, feat), (dker_h, dker), (dbias_h, dbias), (gain_h, gain),
                (nbias_h, nbias), (ubias_h, ubias), (obias_h, obias), (scale_h, scale),
            )
        )
    ]
    for c in own_copy + loads:
        c.start()
    pl.semaphore_wait(barrier, len(near) + 3 * has_up.astype(jnp.int32) + 3 * has_down.astype(jnp.int32))

    def y_copy(w):
        return remote((up, down)[w], wts.at[w, x, mine, :], y_ss.at[w], y_rs.at[w], pair)

    def x1(w, k, i):
        src = (up, down)[w].at[:, pl.ds(0, wide_l)]
        dst = wts.at[w, x, mine, pl.ds(0, wide_l)]
        return remote(src, dst, x1_ss.at[w, k - 1, i], x1_rs.at[w, k - 1, i], at(x + k, z, (y, 1 - y)[i]))

    for w in range(2):
        y_copy(w).start()
        for k in range(1, NX):
            for i in range(2):
                x1(w, k, i).start()

    prow = NY * shard

    def wide(w, zb):
        return wts.at[w, :, pl.ds(pl.multiple_of(zb * prow, prow), prow), pl.ds(0, wide_l)]

    def thin(w, xb, zb):
        return wts.at[w, xb, pl.ds(pl.multiple_of(zb * prow, prow), prow), pl.ds(wide_l, thin_l)]

    def length(w, d):
        return STEPS if w == d else STEPS - 1

    def block(d, s):
        return lax.rem(z + (NZ - s if d == 0 else s), NZ)

    def z1(w, d, s):
        ref = wide(w, block(d, s))
        return remote(ref, ref, z1_ss.at[w, d, s], z1_rs.at[w, d, s], at(x, z + 1 if d == 0 else z - 1))

    def z2(w, d, s):
        ref = thin(w, x, block(d, s))
        return remote(ref, ref, z2_ss.at[w, d, s], z2_rs.at[w, d, s], at(x, z + 1 if d == 0 else z - 1))

    def slot_block(d, s, own_slot):
        return jnp.where(own_slot, z, block(d, s + 1)) if not isinstance(own_slot, bool) else (
            z if own_slot else block(d, s + 1)
        )

    def x2(w, e, d, s, own_slot=False):
        ref = thin(w, x, slot_block(d, s, own_slot))
        return remote(ref, ref, x2_ss.at[w, e], x2_rs.at[w, e, d, s], at(x + 1 - 2 * e, z))

    def xf(w, d, s, own_slot=False):
        ref = thin(w, lax.rem(x + (NX - 1 if d == 0 else 1), NX), slot_block(d, s, own_slot))
        return remote(ref, ref, xf_ss.at[w], xf_rs.at[w], at(x + 1 - 2 * d, z))

    def xd(w, d, s):
        ref = thin(w, x, block(d, s + 1))
        return remote(ref, ref, xf_ss.at[w], xf_rs.at[w], at(x + 2, z))

    def bulk(w, ss, rs):
        ref = wts.at[w, 0, :, pl.ds(wide_l, thin_l)]
        return remote(ref, ref, ss, rs, at(x + 1, z))

    for c in loads[:2]:
        c.wait()
    for a in range(7):
        kers[a, 0:7, :] = dker[a].astype(f32)
    low4 = lax.broadcasted_iota(jnp.int32, (8, chans), 0) < 4

    def pack(q, _):
        v = [feat[4 * q + i].astype(f32) for i in range(4)]
        turned = [pltpu.roll(t, 4, 0) for t in v]
        right = [jnp.where(low4, turned[i], v[i + 1]) for i in (0, 2)]
        left = [jnp.where(low4, v[i], turned[i + 1]) for i in (0, 2)]
        csend[0, q] = jnp.concatenate(right, 0).astype(bf16)
        csend[1, q] = jnp.concatenate(left, 0).astype(bf16)
        return 0

    lax.fori_loop(0, rows // 4, pack, 0)

    last = rows // 4 - 1

    def h_copy(side, c):
        src = csend.at[side, pl.ds(2 * c, 2)]
        dst = crecv.at[side, pl.ds(2 * c + 1, 2)]
        return remote(src, dst, hc_ss.at[side, c], hc_rs.at[side, c], (lat, (east, west)[side]))

    to_down = [
        remote(feat.at[pl.ds(rows - 3, 3)], rrecv.at[0], h_ss.at[0], h_rs.at[0], (lat + 1, lon)),
        remote(csend.at[0, last], crecv.at[0, 0], h_ss.at[1], h_rs.at[1], (lat + 1, east)),
        remote(csend.at[1, last], crecv.at[1, 0], h_ss.at[2], h_rs.at[2], (lat + 1, west)),
    ]
    to_up = [
        remote(feat.at[pl.ds(0, 3)], rrecv.at[1], h_ss.at[3], h_rs.at[3], (lat - 1, lon)),
        remote(csend.at[0, 0], crecv.at[0, last + 2], h_ss.at[4], h_rs.at[4], (lat - 1, east)),
        remote(csend.at[1, 0], crecv.at[1, last + 2], h_ss.at[5], h_rs.at[5], (lat - 1, west)),
    ]

    for c in own_copy:
        c.wait()
    for w in range(2):
        y_copy(w).wait_recv()
        for d in range(2):
            z2(w, d, 0).start()
        for e in range(2):
            x2(w, e, 1 - w, STEPS - 1, True).start()
    for c in range(2):
        for side in range(2):
            h_copy(side, c).start()

    @pl.when(has_down)
    def _():
        for c in to_down:
            c.start()

    @pl.when(has_up)
    def _():
        for c in to_up:
            c.start()

    def widen(h, _):
        v = feat[h].astype(f32)
        for t in range(tiles):
            xpad[t, h + 4, 8:16, :] = v[:, t * 128 : (t + 1) * 128]
        return 0

    lax.fori_loop(0, rows, widen, 0)

    def thin_step(w, s):
        for d in range(2):
            if isinstance(s, int) and s >= length(w, d):
                continue
            z2(w, d, s).wait_recv()
            if not isinstance(s, int) or s + 1 < length(w, d):
                z2(w, d, s + 1).start()
            for e in range(2):
                x2(w, e, d, s).start()
            if isinstance(s, int) and s >= DIRECT:
                xd(w, d, s).start()
        if isinstance(s, int) and s == 0:
            x2(w, 1 - w, 1 - w, STEPS - 1, True).wait_recv()
            xf(w, 1 - w, STEPS - 1, True).start()
        elif not isinstance(s, int) or s <= DIRECT:
            for d in range(2):
                cross_step(w, d, s - 1)

    def cross_step(w, d, s):
        x2(w, d, d, s).wait_recv()
        xf(w, d, s).start()

    def wide_step(w, s):
        for d in range(2):
            if isinstance(s, int) and s >= length(w, d):
                continue
            z1(w, d, s).wait_recv()
            if not isinstance(s, int) or s + 1 < length(w, d):
                z1(w, d, s + 1).start()

    def gathered(w):
        for d in range(2):

            def one(s, _, d=d):
                x2(w, 1 - d, d, s).wait_recv()
                return 0

            lax.fori_loop(0, STEPS, one, 0)
            for s in range(DIRECT, length(w, d)):
                x2(w, d, d, s).wait_recv()
        bulk(w, xf_ss.at[w], xf_rs.at[w]).wait_recv()

    for w in range(2):
        for k in range(1, NX):
            for i in range(2):
                x1(w, k, i).wait_recv()
        for d in range(2):
            z1(w, d, 0).start()
    for side in range(2):
        h_copy(side, 2).start()
    for s in range(EARLY + 1):
        for w in range(2):
            thin_step(w, s)
            if s > 0:
                wide_step(w, s - 1)
        if s == 0:
            for side in range(2):
                h_copy(side, 3).start()
    for c in loads[2:]:
        c.wait()

    def place(q):
        for side, lo in ((0, 4), (1, 16)):
            v = crecv[side, q].astype(f32)
            for i in range(4):
                for t in range(tiles):
                    xpad[t, 4 * q + i, lo : lo + 4, :] = v[4 * i : 4 * i + 4, t * 128 : (t + 1) * 128]

    def chunk_in(c):
        for side in range(2):
            h_copy(side, c).wait_recv()

        def one(i, _):
            place(2 * c + 1 + i)
            return 0

        lax.fori_loop(0, 2, one, 0)

    chunk_in(0)

    def margin(present, copies, row0, q, slot):
        @pl.when(present)
        def _():
            for c in copies:
                c.wait_recv()
            place(q)
            for r in range(3):
                v = rrecv[slot, r].astype(f32)
                for t in range(tiles):
                    xpad[t, row0 + r, 8:16, :] = v[:, t * 128 : (t + 1) * 128]

        @pl.when(jnp.logical_not(present))
        def _():
            for r in range(3):
                for t in range(tiles):
                    xpad[t, row0 + r] = jnp.zeros((24, 128), f32)

    margin(has_up, to_down, 1, 0, 0)

    def conv_tile(rb, t):
        lanes = pl.ds(pl.multiple_of(t * 128, 128), 128)
        acc = [jnp.broadcast_to(dbias[:, lanes], (8, 128)) for _ in range(8)]
        for b in range(7):
            win = [xpad[t, rb * 8 + 1 + r, 5 + b : 13 + b, :] for r in range(14)]
            for a in range(7):
                k = jnp.broadcast_to(kers[a, b : b + 1, lanes], (8, 128))
                for o in range(8):
                    acc[o] = acc[o] + win[o + a] * k
        for o in range(8):
            conv[pl.ds(pl.multiple_of((rb * 8 + o) * 8, 8), 8), lanes] = acc[o]

    def norm_group(rb, g):
        px = pl.ds(pl.multiple_of(rb * chunk + g * 16, 16), 16)
        v = conv[px, :]
        v = v - jnp.mean(v, axis=-1, keepdims=True)
        var = jnp.mean(v * v, axis=-1, keepdims=True)
        v = v * lax.rsqrt(var + 1e-06) * gain[...] + nbias[...]
        acts[lat, px, :] = v.astype(bf16)

    def act(slot, c):
        return acts.at[slot, pl.ds(pl.multiple_of(c * chunk, chunk), chunk), :]

    def a_sib(c):
        return remote(act(lat, c), act(lat, c), a_ss.at[0, c], a_rs.at[0, c], sib)

    def a_crs(c):
        return remote(act(lat, c), act(lat, c), a_ss.at[1, c], a_rs.at[1, c], crs)

    def a_fwd(c):
        return remote(act(far, c), act(far, c), a_ss.at[2, c], a_rs.at[2, c], sib)

    def conv_block(rb, _):
        @pl.when(rb < blocks - 1)
        def _():
            chunk_in(rb + 1)

        @pl.when(rb == blocks - 1)
        def _():
            margin(has_down, to_up, rows + 4, last + 2, 1)

        def run(t, _):
            conv_tile(rb, t)
            return 0

        lax.fori_loop(0, tiles // 2, run, 0)
        thin_step(0, rb + EARLY + 1)
        wide_step(0, rb + EARLY)
        lax.fori_loop(tiles // 2, tiles, run, 0)

        def run_norm(g, _):
            norm_group(rb, g)
            return 0

        lax.fori_loop(0, chunk // 16, run_norm, 0)
        a_crs(rb).start()
        a_sib(rb).start()
        thin_step(1, rb + EARLY + 1)
        wide_step(1, rb + EARLY)
        return 0

    lax.fori_loop(0, blocks, conv_block, 0)

    def forward(c):
        a_crs(c).wait_recv()
        a_fwd(c).start()

    pending = list(range(blocks))
    for s in range(EARLY + blocks, STEPS + 1):
        for w in range(2):
            if s + 1 < STEPS:
                thin_step(w, s + 1)
            if s < STEPS:
                wide_step(w, s)
            if w == 0 and pending:
                forward(pending.pop(0))
    for c in pending:
        forward(c)
    gathered(0)

    def pointwise(q, h):
        def one(n, _):
            lanes = pl.ds(pl.multiple_of(n * 256, 256), 256)
            wt = wts[0, :, :, lanes].reshape(chans, 256)
            pre = jnp.dot(acts[q], wt, preferred_element_type=f32) + ubias[:, lanes]
            act_ = 0.5 * pre * (1.0 + lax.erf(pre * 0.7071067811865476))
            hid[h, :, lanes] = act_.astype(bf16)
            return 0

        lax.fori_loop(0, hidden // 256, one, 0)

    def project(n, h):
        return lax.dot_general(hid[h], wts[1, n], (((1,), (1,)), ((), ())), preferred_element_type=f32)

    def o_copy(kind, n):
        src, dst, device = ((s_sib, r_sib, sib), (s_mid, r_mid, crs), (s_crs, r_crs, sib))[kind]
        return remote(src.at[n], dst.at[n], o_ss.at[kind, n], o_rs.at[kind, n], device)

    parts = NX
    for c in range(blocks):
        a_sib(c).wait_recv()
        a_fwd(c).wait_recv()

    pointwise(far_flip, 0)
    pointwise(far, 1)
    gathered(1)

    def first_part(n):
        s_sib[n] = project(n, 0).astype(bf16)
        o_copy(0, n).start()

    def second_part(n):
        total = project(n, 1)
        o_copy(0, n).wait_recv()
        s_mid[n] = (total + r_sib[n].astype(f32)).astype(bf16)
        o_copy(1, n).start()

    first_part(0)

    def both_parts(n, _):
        first_part(n + 1)
        second_part(n)
        return 0

    lax.fori_loop(0, parts - 1, both_parts, 0)
    second_part(parts - 1)

    pointwise(flip, 0)

    def third_part(n, _):
        s_crs[n] = project(n, 0).astype(bf16)
        o_copy(2, n).start()
        return 0

    lax.fori_loop(0, parts, third_part, 0)

    pointwise(lat, 1)

    def own_part(n, _):
        own[n] = project(n, 1)
        return 0

    lax.fori_loop(0, parts, own_part, 0)

    def finish(n, _):
        width = chans // parts
        lanes = pl.ds(pl.multiple_of(n * width, width), width)
        o_copy(2, n).wait_recv()
        part = own[n] + r_crs[n].astype(f32)
        o_copy(1, n).wait_recv()
        part = part + r_mid[n].astype(f32)
        part = scale[:, lanes] * (part + obias[:, lanes])
        res = feat[:, :, lanes].astype(f32) + part.reshape(rows, cols, width)
        out[:, :, lanes] = res.astype(bf16)
        return 0

    lax.fori_loop(0, parts, finish, 0)

    for w in range(2):
        y_copy(w).wait_send()
        for k in range(1, NX):
            for i in range(2):
                x1(w, k, i).wait_send()
        for e in range(2):
            bulk(w, x2_ss.at[w, e], xf_rs.at[w]).wait_send()
        bulk(w, xf_ss.at[w], xf_rs.at[w]).wait_send()
        for d in range(2):

            def gone(s, _, w=w, d=d):
                z1(w, d, s).wait_send()
                z2(w, d, s).wait_send()
                return 0

            lax.fori_loop(0, length(w, d), gone, 0)
    for side in range(2):
        for c in range(blocks):
            h_copy(side, c).wait_send()

    @pl.when(has_down)
    def _():
        for c in to_down:
            c.wait_send()

    @pl.when(has_up)
    def _():
        for c in to_up:
            c.wait_send()

    for c in range(blocks):
        a_sib(c).wait_send()
        a_crs(c).wait_send()
        a_fwd(c).wait_send()
    for n in range(parts):
        for kind in range(3):
            o_copy(kind, n).wait_send()


def local(
    features, depth_kernel, depth_bias, norm_gain, norm_bias, up_weight, up_bias, down_weight, down_bias, layer_scale
):
    rows, cols, chans = features.shape
    shard, hidden = up_weight.shape
    pixels = rows * cols
    bf16, f32 = jnp.bfloat16, jnp.float32
    vmem, dma = pltpu.VMEM, pltpu.SemaphoreType.DMA
    blocks = rows // 8
    flat = lambda v: v.reshape(1, -1)
    spec = pl.BlockSpec(memory_space=pltpu.VMEM)
    piece = (NX, pixels, chans // NX)
    return pl.pallas_call(
        kernel,
        out_shape=jax.ShapeDtypeStruct(features.shape, features.dtype),
        in_specs=[pl.BlockSpec(memory_space=pltpu.HBM)] * 10,
        out_specs=spec,
        scratch_shapes=[
            vmem(features.shape, bf16),
            vmem(depth_kernel.shape, bf16),
            vmem((1, chans), f32),
            vmem((1, chans), f32),
            vmem((1, chans), f32),
            vmem((1, hidden), f32),
            vmem((1, chans), f32),
            vmem((1, chans), f32),
            vmem((2, NX, chans // NX, hidden), bf16),
            vmem((chans // 128, rows + 8, 24, 128), f32),
            vmem((7, 8, chans), f32),
            vmem((pixels, chans), f32),
            vmem((2, rows // 4, 16, chans), bf16),
            vmem((2, rows // 4 + 2, 16, chans), bf16),
            vmem((2, 3, cols, chans), bf16),
            vmem((4, pixels, chans), bf16),
            vmem((2, pixels, hidden), bf16),
            vmem(piece, f32),
            vmem(piece, bf16),
            vmem(piece, bf16),
            vmem(piece, bf16),
            vmem(piece, bf16),
            vmem(piece, bf16),
            vmem(piece, bf16),
            dma((8,)), dma((2,)),
            dma((2,)), dma((2,)),
            dma((6,)), dma((6,)),
            dma((2, blocks)), dma((2, blocks)),
            dma((2, NX - 1, 2)), dma((2, NX - 1, 2)),
            dma((2, 2)), dma((2, 2, 2, STEPS)),
            dma((2,)), dma((2,)),
            dma((2, 2, STEPS)), dma((2, 2, STEPS)),
            dma((2, 2, STEPS)), dma((2, 2, STEPS)),
            dma((3, blocks)), dma((3, blocks)),
            dma((3, NX)), dma((3, NX)),
        ],
        compiler_params=pltpu.CompilerParams(
            collective_id=0, has_side_effects=True, vmem_limit_bytes=63 << 20
        ),
    )(
        features, depth_kernel, flat(depth_bias), flat(norm_gain), flat(norm_bias), up_weight, flat(up_bias),
        down_weight, flat(down_bias), flat(layer_scale),
    )


def solution(mesh):
    placed = (
        P("lat", "lon", None), P(), P(), P(), P(), P("lon", "lat"), P("lat"), P("lon", "lat"), P(), P(),
    )
    return jax.shard_map(
        local, mesh=mesh, in_specs=placed, out_specs=P("lat", "lon", None), check_vma=False
    )
```

```python
import functools

import jax
import jax.numpy as jnp
from jax import lax
from jax.experimental import pallas as pl
from jax.experimental.pallas import tpu as pltpu
from jax.sharding import PartitionSpec as P

MESH = pl.DeviceIdType.MESH
NX, NZ, NY = 4, 16, 2
STEPS = NZ // 2
HOPS = STEPS // 2
DIRECT = STEPS - 2


def remote(src, dst, send_sem, recv_sem, device):
    return pltpu.make_async_remote_copy(
        src_ref=src, dst_ref=dst, send_sem=send_sem, recv_sem=recv_sem, device_id=device, device_id_type=MESH
    )


def kernel(
    feat_h, dker_h, dbias_h, gain_h, nbias_h, up, ubias_h, down, obias_h, scale_h,
    out,
    feat, dker, dbias, gain, nbias, ubias, obias, scale,
    wts, xpad, kers, conv, csend, crecv, rrecv, acts, hid, own, s_sib, s_mid, s_crs, r_sib, r_mid, r_crs,
    in_s, own_s, y_ss, y_rs, h_ss, h_rs, hc_ss, hc_rs, x1_ss, x1_rs, x2_ss, x2_rs, xf_ss, xf_rs, z1_ss, z1_rs, z2_ss, z2_rs, a_ss, a_rs, o_ss, o_rs,
):
    f32, bf16 = jnp.float32, jnp.bfloat16
    rows, cols, chans = feat.shape
    hidden = up.shape[1]
    tiles = chans // 128
    wide_l = hidden // 8
    thin_l = hidden - wide_l
    blocks = rows // 8
    chunk = 8 * cols
    pixels = rows * cols
    n_lon = NX * NZ * NY
    lat = lax.axis_index("lat")
    lon = lax.axis_index("lon")
    y = lax.rem(lon, NY)
    z = lax.rem(lon // NY, NZ)
    x = lon // (NY * NZ)

    def at(x_, z_, y_=y):
        return (lat, (lax.rem(x_ + NX, NX) * NZ + lax.rem(z_ + NZ, NZ)) * NY + y_)

    flip = lat + 1 - 2 * lax.rem(lat, 2)
    far = lax.rem(lat + 2, 4)
    far_flip = lax.rem(flip + 2, 4)
    pair_lon = lon + 1 - 2 * y
    pair = (lat, pair_lon)
    sib = (flip, lon)
    crs = (far, pair_lon)
    east = lax.rem(lon + 1, n_lon)
    west = lax.rem(lon + n_lon - 1, n_lon)
    has_up = lat > 0
    has_down = lat < 3

    barrier = pltpu.get_barrier_semaphore()

    def hello(device):
        pl.semaphore_signal(barrier, inc=1, device_id=device, device_id_type=MESH)

    near = [pair, sib, crs, (lat, east), (lat, west), at(x, z + 1), at(x, z - 1), at(x, z + 2), at(x, z - 2)]
    near += [at(x + k, z, y_) for k in range(1, NX) for y_ in (y, 1 - y)]
    for device in near:
        hello(device)

    @pl.when(has_up)
    def _():
        for lon_ in (west, lon, east):
            hello((lat - 1, lon_))

    @pl.when(has_down)
    def _():
        for lon_ in (west, lon, east):
            hello((lat + 1, lon_))

    shard = up.shape[0]
    mine = pl.ds(pl.multiple_of((z * NY + y) * shard, shard), shard)
    own_copy = [pltpu.make_async_copy((up, down)[w], wts.at[w, x, mine, :], own_s.at[w]) for w in range(2)]
    loads = [
        pltpu.make_async_copy(a, b, in_s.at[i])
        for i, (a, b) in enumerate(
            (
                (feat_h, feat), (dker_h, dker), (dbias_h, dbias), (gain_h, gain),
                (nbias_h, nbias), (ubias_h, ubias), (obias_h, obias), (scale_h, scale),
            )
        )
    ]
    for c in own_copy + loads:
        c.start()
    pl.semaphore_wait(barrier, len(near) + 3 * has_up.astype(jnp.int32) + 3 * has_down.astype(jnp.int32))

    def y_copy(w):
        return remote((up, down)[w], wts.at[w, x, mine, :], y_ss.at[w], y_rs.at[w], pair)

    def x1(w, k, i):
        src = (up, down)[w].at[:, pl.ds(0, wide_l)]
        dst = wts.at[w, x, mine, pl.ds(0, wide_l)]
        return remote(src, dst, x1_ss.at[w, k - 1, i], x1_rs.at[w, k - 1, i], at(x + k, z, (y, 1 - y)[i]))

    for w in range(2):
        y_copy(w).start()
        for k in range(1, NX):
            for i in range(2):
                x1(w, k, i).start()

    prow = NY * shard

    def wide(w, zb):
        return wts.at[w, :, pl.ds(pl.multiple_of(zb * prow, prow), prow), pl.ds(0, wide_l)]

    def thin(w, xb, zb):
        return wts.at[w, xb, pl.ds(pl.multiple_of(zb * prow, prow), prow), pl.ds(wide_l, thin_l)]

    def length(w, d):
        return STEPS if w == d else STEPS - 1

    def block(d, s):
        return lax.rem(z + (NZ - s if d == 0 else s), NZ)

    def z1(w, d, s, j):
        ref = wide(w, block(d, 2 * s))
        return remote(ref, ref, z1_ss.at[w, d, s, j], z1_rs.at[w, d, s, j], at(x, z + (1 + j) * (1 - 2 * d)))

    def z2(w, d, s, j):
        ref = thin(w, x, block(d, 2 * s))
        return remote(ref, ref, z2_ss.at[w, d, s, j], z2_rs.at[w, d, s, j], at(x, z + (1 + j) * (1 - 2 * d)))

    def reach(w, d, s):
        return [j for j in (1, 0) if s < HOPS and 2 * s + j < length(w, d)]

    def slot_block(d, s, own_slot):
        return jnp.where(own_slot, z, block(d, s + 1)) if not isinstance(own_slot, bool) else (
            z if own_slot else block(d, s + 1)
        )

    def x2(w, e, d, s, own_slot=False):
        ref = thin(w, x, slot_block(d, s, own_slot))
        return remote(ref, ref, x2_ss.at[w, e], x2_rs.at[w, e, d, s], at(x + 1 - 2 * e, z))

    def xf(w, d, s, own_slot=False):
        ref = thin(w, lax.rem(x + (NX - 1 if d == 0 else 1), NX), slot_block(d, s, own_slot))
        return remote(ref, ref, xf_ss.at[w], xf_rs.at[w], at(x + 1 - 2 * d, z))

    def xd(w, d, s):
        ref = thin(w, x, block(d, s + 1))
        return remote(ref, ref, xf_ss.at[w], xf_rs.at[w], at(x + 2, z))

    def bulk(w, ss, rs):
        ref = wts.at[w, 0, :, pl.ds(wide_l, thin_l)]
        return remote(ref, ref, ss, rs, at(x + 1, z))

    for c in loads[:2]:
        c.wait()
    for a in range(7):
        kers[a, 0:7, :] = dker[a].astype(f32)
    low4 = lax.broadcasted_iota(jnp.int32, (8, chans), 0) < 4

    def pack(q, _):
        v = [feat[4 * q + i].astype(f32) for i in range(4)]
        turned = [pltpu.roll(t, 4, 0) for t in v]
        right = [jnp.where(low4, turned[i], v[i + 1]) for i in (0, 2)]
        left = [jnp.where(low4, v[i], turned[i + 1]) for i in (0, 2)]
        csend[0, q] = jnp.concatenate(right, 0).astype(bf16)
        csend[1, q] = jnp.concatenate(left, 0).astype(bf16)
        return 0

    lax.fori_loop(0, rows // 4, pack, 0)

    last = rows // 4 - 1

    def h_copy(side, c):
        src = csend.at[side, pl.ds(2 * c, 2)]
        dst = crecv.at[side, pl.ds(2 * c + 1, 2)]
        return remote(src, dst, hc_ss.at[side, c], hc_rs.at[side, c], (lat, (east, west)[side]))

    to_down = [
        remote(feat.at[pl.ds(rows - 3, 3)], rrecv.at[0], h_ss.at[0], h_rs.at[0], (lat + 1, lon)),
        remote(csend.at[0, last], crecv.at[0, 0], h_ss.at[1], h_rs.at[1], (lat + 1, east)),
        remote(csend.at[1, last], crecv.at[1, 0], h_ss.at[2], h_rs.at[2], (lat + 1, west)),
    ]
    to_up = [
        remote(feat.at[pl.ds(0, 3)], rrecv.at[1], h_ss.at[3], h_rs.at[3], (lat - 1, lon)),
        remote(csend.at[0, 0], crecv.at[0, last + 2], h_ss.at[4], h_rs.at[4], (lat - 1, east)),
        remote(csend.at[1, 0], crecv.at[1, last + 2], h_ss.at[5], h_rs.at[5], (lat - 1, west)),
    ]

    for c in own_copy:
        c.wait()
    for w in range(2):
        y_copy(w).wait_recv()
        for d in range(2):
            for j in reach(w, d, 0):
                z2(w, d, 0, j).start()
        for e in range(2):
            x2(w, e, 1 - w, STEPS - 1, True).start()
    for c in range(2):
        for side in range(2):
            h_copy(side, c).start()

    @pl.when(has_down)
    def _():
        for c in to_down:
            c.start()

    @pl.when(has_up)
    def _():
        for c in to_up:
            c.start()

    def widen(h, _):
        v = feat[h].astype(f32)
        for t in range(tiles):
            xpad[t, h + 4, 8:16, :] = v[:, t * 128 : (t + 1) * 128]
        return 0

    lax.fori_loop(0, rows, widen, 0)

    def thin_step(w, s):
        for d in range(2):
            for j in reach(w, d, s):
                z2(w, d, s, j).wait_recv()
                if j == 1:
                    for i in reach(w, d, s + 1):
                        z2(w, d, s + 1, i).start()
                for e in range(2):
                    x2(w, e, d, 2 * s + j).start()
                if 2 * s + j >= DIRECT:
                    xd(w, d, 2 * s + j).start()
        if s == 0:
            x2(w, 1 - w, 1 - w, STEPS - 1, True).wait_recv()
            xf(w, 1 - w, STEPS - 1, True).start()
        else:
            for d in range(2):
                for j in range(2):
                    cross_step(w, d, 2 * s - 2 + j)

    def cross_step(w, d, s):
        x2(w, d, d, s).wait_recv()
        xf(w, d, s).start()

    def wide_step(w, s):
        for d in range(2):
            for j in reach(w, d, s):
                z1(w, d, s, j).wait_recv()
                if j == 1:
                    for i in reach(w, d, s + 1):
                        z1(w, d, s + 1, i).start()

    def gathered(w):
        for d in range(2):

            def one(s, _, d=d):
                x2(w, 1 - d, d, s).wait_recv()
                return 0

            lax.fori_loop(0, STEPS, one, 0)
            for s in range(DIRECT, length(w, d)):
                x2(w, d, d, s).wait_recv()
        bulk(w, xf_ss.at[w], xf_rs.at[w]).wait_recv()

    for w in range(2):
        for k in range(1, NX):
            for i in range(2):
                x1(w, k, i).wait_recv()
        for d in range(2):
            for j in reach(w, d, 0):
                z1(w, d, 0, j).start()
    for side in range(2):
        h_copy(side, 2).start()
    for w in range(2):
        thin_step(w, 0)
    for side in range(2):
        h_copy(side, 3).start()
    for w in range(2):
        wide_step(w, 0)
        thin_step(w, 1)
    for c in loads[2:]:
        c.wait()

    def place(q):
        for side, lo in ((0, 4), (1, 16)):
            v = crecv[side, q].astype(f32)
            for i in range(4):
                for t in range(tiles):
                    xpad[t, 4 * q + i, lo : lo + 4, :] = v[4 * i : 4 * i + 4, t * 128 : (t + 1) * 128]

    def chunk_in(c):
        for side in range(2):
            h_copy(side, c).wait_recv()

        def one(i, _):
            place(2 * c + 1 + i)
            return 0

        lax.fori_loop(0, 2, one, 0)

    chunk_in(0)

    def margin(present, copies, row0, q, slot):
        @pl.when(present)
        def _():
            for c in copies:
                c.wait_recv()
            place(q)
            for r in range(3):
                v = rrecv[slot, r].astype(f32)
                for t in range(tiles):
                    xpad[t, row0 + r, 8:16, :] = v[:, t * 128 : (t + 1) * 128]

        @pl.when(jnp.logical_not(present))
        def _():
            for r in range(3):
                for t in range(tiles):
                    xpad[t, row0 + r] = jnp.zeros((24, 128), f32)

    margin(has_up, to_down, 1, 0, 0)

    def conv_tile(rb, t):
        lanes = pl.ds(pl.multiple_of(t * 128, 128), 128)
        acc = [jnp.broadcast_to(dbias[:, lanes], (8, 128)) for _ in range(8)]
        for b in range(7):
            win = [xpad[t, rb * 8 + 1 + r, 5 + b : 13 + b, :] for r in range(14)]
            for a in range(7):
                k = jnp.broadcast_to(kers[a, b : b + 1, lanes], (8, 128))
                for o in range(8):
                    acc[o] = acc[o] + win[o + a] * k
        for o in range(8):
            conv[pl.ds(pl.multiple_of((rb * 8 + o) * 8, 8), 8), lanes] = acc[o]

    def norm_group(rb, g):
        px = pl.ds(pl.multiple_of(rb * chunk + g * 16, 16), 16)
        v = conv[px, :]
        v = v - jnp.mean(v, axis=-1, keepdims=True)
        var = jnp.mean(v * v, axis=-1, keepdims=True)
        v = v * lax.rsqrt(var + 1e-06) * gain[...] + nbias[...]
        acts[lat, px, :] = v.astype(bf16)

    def act(slot, c):
        return acts.at[slot, pl.ds(pl.multiple_of(c * chunk, chunk), chunk), :]

    def a_sib(c):
        return remote(act(lat, c), act(lat, c), a_ss.at[0, c], a_rs.at[0, c], sib)

    def a_crs(c):
        return remote(act(lat, c), act(lat, c), a_ss.at[1, c], a_rs.at[1, c], crs)

    def a_fwd(c):
        return remote(act(far, c), act(far, c), a_ss.at[2, c], a_rs.at[2, c], sib)

    def turn(w, rb):
        for i, (step, s) in enumerate(((wide_step, 1), (thin_step, 2), (wide_step, 2), (thin_step, 3))):

            @pl.when(rb == i)
            def _(step=step, s=s):
                step(w, s)

    def conv_block(rb, _):
        @pl.when(rb < blocks - 1)
        def _():
            chunk_in(rb + 1)

        @pl.when(rb == blocks - 1)
        def _():
            margin(has_down, to_up, rows + 4, last + 2, 1)

        def run(t, _):
            conv_tile(rb, t)
            return 0

        lax.fori_loop(0, tiles // 2, run, 0)
        turn(0, rb)
        lax.fori_loop(tiles // 2, tiles, run, 0)

        def run_norm(g, _):
            norm_group(rb, g)
            return 0

        lax.fori_loop(0, chunk // 16, run_norm, 0)
        a_crs(rb).start()
        a_sib(rb).start()
        turn(1, rb)
        return 0

    lax.fori_loop(0, blocks, conv_block, 0)

    def forward(c):
        a_crs(c).wait_recv()
        a_fwd(c).start()

    for c in range(blocks - 1):
        forward(c)
    for w in range(2):
        wide_step(w, HOPS - 1)
    forward(blocks - 1)
    gathered(0)

    def pointwise(q, h):
        def one(n, _):
            lanes = pl.ds(pl.multiple_of(n * 256, 256), 256)
            wt = wts[0, :, :, lanes].reshape(chans, 256)
            pre = jnp.dot(acts[q], wt, preferred_element_type=f32) + ubias[:, lanes]
            act_ = 0.5 * pre * (1.0 + lax.erf(pre * 0.7071067811865476))
            hid[h, :, lanes] = act_.astype(bf16)
            return 0

        lax.fori_loop(0, hidden // 256, one, 0)

    def project(n, h):
        return lax.dot_general(hid[h], wts[1, n], (((1,), (1,)), ((), ())), preferred_element_type=f32)

    def o_copy(kind, n):
        src, dst, device = ((s_sib, r_sib, sib), (s_mid, r_mid, crs), (s_crs, r_crs, sib))[kind]
        return remote(src.at[n], dst.at[n], o_ss.at[kind, n], o_rs.at[kind, n], device)

    parts = NX
    for c in range(blocks):
        a_sib(c).wait_recv()
        a_fwd(c).wait_recv()

    pointwise(far_flip, 0)
    pointwise(far, 1)
    gathered(1)

    def first_part(n):
        s_sib[n] = project(n, 0).astype(bf16)
        o_copy(0, n).start()

    def second_part(n):
        total = project(n, 1)
        o_copy(0, n).wait_recv()
        s_mid[n] = (total + r_sib[n].astype(f32)).astype(bf16)
        o_copy(1, n).start()

    first_part(0)

    def both_parts(n, _):
        first_part(n + 1)
        second_part(n)
        return 0

    lax.fori_loop(0, parts - 1, both_parts, 0)
    second_part(parts - 1)

    pointwise(flip, 0)

    def third_part(n, _):
        s_crs[n] = project(n, 0).astype(bf16)
        o_copy(2, n).start()
        return 0

    lax.fori_loop(0, parts, third_part, 0)

    pointwise(lat, 1)

    def own_part(n, _):
        own[n] = project(n, 1)
        return 0

    lax.fori_loop(0, parts, own_part, 0)

    def finish(n, _):
        width = chans // parts
        lanes = pl.ds(pl.multiple_of(n * width, width), width)
        o_copy(2, n).wait_recv()
        part = own[n] + r_crs[n].astype(f32)
        o_copy(1, n).wait_recv()
        part = part + r_mid[n].astype(f32)
        part = scale[:, lanes] * (part + obias[:, lanes])
        res = feat[:, :, lanes].astype(f32) + part.reshape(rows, cols, width)
        out[:, :, lanes] = res.astype(bf16)
        return 0

    lax.fori_loop(0, parts, finish, 0)

    for w in range(2):
        y_copy(w).wait_send()
        for k in range(1, NX):
            for i in range(2):
                x1(w, k, i).wait_send()
        for e in range(2):
            bulk(w, x2_ss.at[w, e], xf_rs.at[w]).wait_send()
        bulk(w, xf_ss.at[w], xf_rs.at[w]).wait_send()
        for d in range(2):

            for s in range(HOPS):
                for j in reach(w, d, s):
                    z1(w, d, s, j).wait_send()
                    z2(w, d, s, j).wait_send()
    for side in range(2):
        for c in range(blocks):
            h_copy(side, c).wait_send()

    @pl.when(has_down)
    def _():
        for c in to_down:
            c.wait_send()

    @pl.when(has_up)
    def _():
        for c in to_up:
            c.wait_send()

    for c in range(blocks):
        a_sib(c).wait_send()
        a_crs(c).wait_send()
        a_fwd(c).wait_send()
    for n in range(parts):
        for kind in range(3):
            o_copy(kind, n).wait_send()


def local(
    features, depth_kernel, depth_bias, norm_gain, norm_bias, up_weight, up_bias, down_weight, down_bias, layer_scale
):
    rows, cols, chans = features.shape
    shard, hidden = up_weight.shape
    pixels = rows * cols
    bf16, f32 = jnp.bfloat16, jnp.float32
    vmem, dma = pltpu.VMEM, pltpu.SemaphoreType.DMA
    blocks = rows // 8
    flat = lambda v: v.reshape(1, -1)
    spec = pl.BlockSpec(memory_space=pltpu.VMEM)
    piece = (NX, pixels, chans // NX)
    return pl.pallas_call(
        kernel,
        out_shape=jax.ShapeDtypeStruct(features.shape, features.dtype),
        in_specs=[pl.BlockSpec(memory_space=pltpu.HBM)] * 10,
        out_specs=spec,
        scratch_shapes=[
            vmem(features.shape, bf16),
            vmem(depth_kernel.shape, bf16),
            vmem((1, chans), f32),
            vmem((1, chans), f32),
            vmem((1, chans), f32),
            vmem((1, hidden), f32),
            vmem((1, chans), f32),
            vmem((1, chans), f32),
            vmem((2, NX, chans // NX, hidden), bf16),
            vmem((chans // 128, rows + 8, 24, 128), f32),
            vmem((7, 8, chans), f32),
            vmem((pixels, chans), f32),
            vmem((2, rows // 4, 16, chans), bf16),
            vmem((2, rows // 4 + 2, 16, chans), bf16),
            vmem((2, 3, cols, chans), bf16),
            vmem((4, pixels, chans), bf16),
            vmem((2, pixels, hidden), bf16),
            vmem(piece, f32),
            vmem(piece, bf16),
            vmem(piece, bf16),
            vmem(piece, bf16),
            vmem(piece, bf16),
            vmem(piece, bf16),
            vmem(piece, bf16),
            dma((8,)), dma((2,)),
            dma((2,)), dma((2,)),
            dma((6,)), dma((6,)),
            dma((2, blocks)), dma((2, blocks)),
            dma((2, NX - 1, 2)), dma((2, NX - 1, 2)),
            dma((2, 2)), dma((2, 2, 2, STEPS)),
            dma((2,)), dma((2,)),
            dma((2, 2, HOPS, 2)), dma((2, 2, HOPS, 2)),
            dma((2, 2, HOPS, 2)), dma((2, 2, HOPS, 2)),
            dma((3, blocks)), dma((3, blocks)),
            dma((3, NX)), dma((3, NX)),
        ],
        compiler_params=pltpu.CompilerParams(
            collective_id=0, has_side_effects=True, vmem_limit_bytes=63 << 20
        ),
    )(
        features, depth_kernel, flat(depth_bias), flat(norm_gain), flat(norm_bias), up_weight, flat(up_bias),
        down_weight, flat(down_bias), flat(layer_scale),
    )


def solution(mesh):
    placed = (
        P("lat", "lon", None), P(), P(), P(), P(), P("lon", "lat"), P("lat"), P("lon", "lat"), P(), P(),
    )
    return jax.shard_map(
        local, mesh=mesh, in_specs=placed, out_specs=P("lat", "lon", None), check_vma=False
    )
```

```python
import functools

import jax
import jax.numpy as jnp
from jax import lax
from jax.experimental import pallas as pl
from jax.experimental.pallas import tpu as pltpu
from jax.sharding import PartitionSpec as P

MESH = pl.DeviceIdType.MESH
NX, NZ, NY = 4, 16, 2
STEPS = NZ // 2
EARLY = 1
DIRECT = STEPS - 2


def remote(src, dst, send_sem, recv_sem, device):
    return pltpu.make_async_remote_copy(
        src_ref=src, dst_ref=dst, send_sem=send_sem, recv_sem=recv_sem, device_id=device, device_id_type=MESH
    )


def kernel(
    feat_h, dker_h, dbias_h, gain_h, nbias_h, up, ubias_h, down, obias_h, scale_h,
    out,
    feat, dker, dbias, gain, nbias, ubias, obias, scale,
    wts, xpad, kers, conv, csend, crecv, rrecv, acts, hid, own, s_sib, s_mid, s_crs, r_sib, r_mid, r_crs,
    in_s, own_s, y_ss, y_rs, h_ss, h_rs, hc_ss, hc_rs, x1_ss, x1_rs, x2_ss, x2_rs, xf_ss, xf_rs, z1_ss, z1_rs, z2_ss, z2_rs, a_ss, a_rs, o_ss, o_rs,
):
    f32, bf16 = jnp.float32, jnp.bfloat16
    rows, cols, chans = feat.shape
    hidden = up.shape[1]
    tiles = chans // 128
    wide_l = hidden // 8
    thin_l = hidden - wide_l
    blocks = rows // 8
    chunk = 8 * cols
    pixels = rows * cols
    n_lon = NX * NZ * NY
    lat = lax.axis_index("lat")
    lon = lax.axis_index("lon")
    y = lax.rem(lon, NY)
    z = lax.rem(lon // NY, NZ)
    x = lon // (NY * NZ)

    def at(x_, z_, y_=y):
        return (lat, (lax.rem(x_ + NX, NX) * NZ + lax.rem(z_ + NZ, NZ)) * NY + y_)

    flip = lat + 1 - 2 * lax.rem(lat, 2)
    far = lax.rem(lat + 2, 4)
    far_flip = lax.rem(flip + 2, 4)
    pair_lon = lon + 1 - 2 * y
    pair = (lat, pair_lon)
    sib = (flip, lon)
    crs = (far, pair_lon)
    east = lax.rem(lon + 1, n_lon)
    west = lax.rem(lon + n_lon - 1, n_lon)
    has_up = lat > 0
    has_down = lat < 3

    barrier = pltpu.get_barrier_semaphore()

    def hello(device):
        pl.semaphore_signal(barrier, inc=1, device_id=device, device_id_type=MESH)

    near = [pair, sib, crs, (lat, east), (lat, west), at(x, z + 1), at(x, z - 1)]
    near += [at(x + k, z, y_) for k in range(1, NX) for y_ in (y, 1 - y)]
    for device in near:
        hello(device)

    @pl.when(has_up)
    def _():
        for lon_ in (west, lon, east):
            hello((lat - 1, lon_))

    @pl.when(has_down)
    def _():
        for lon_ in (west, lon, east):
            hello((lat + 1, lon_))

    shard = up.shape[0]
    mine = pl.ds(pl.multiple_of((z * NY + y) * shard, shard), shard)
    own_copy = [pltpu.make_async_copy((up, down)[w], wts.at[w, x, mine, :], own_s.at[w]) for w in range(2)]
    loads = [
        pltpu.make_async_copy(a, b, in_s.at[i])
        for i, (a, b) in enumerate(
            (
                (feat_h, feat), (dker_h, dker), (dbias_h, dbias), (gain_h, gain),
                (nbias_h, nbias), (ubias_h, ubias), (obias_h, obias), (scale_h, scale),
            )
        )
    ]
    for c in own_copy + loads:
        c.start()
    pl.semaphore_wait(barrier, len(near) + 3 * has_up.astype(jnp.int32) + 3 * has_down.astype(jnp.int32))

    def y_copy(w):
        return remote((up, down)[w], wts.at[w, x, mine, :], y_ss.at[w], y_rs.at[w], pair)

    def x1(w, k, i):
        src = (up, down)[w].at[:, pl.ds(0, wide_l)]
        dst = wts.at[w, x, mine, pl.ds(0, wide_l)]
        return remote(src, dst, x1_ss.at[w, k - 1, i], x1_rs.at[w, k - 1, i], at(x + k, z, (y, 1 - y)[i]))

    for w in range(2):
        y_copy(w).start()
        for k in range(1, NX):
            for i in range(2):
                x1(w, k, i).start()

    prow = NY * shard

    def wide(w, zb):
        return wts.at[w, :, pl.ds(pl.multiple_of(zb * prow, prow), prow), pl.ds(0, wide_l)]

    def thin(w, xb, zb):
        return wts.at[w, xb, pl.ds(pl.multiple_of(zb * prow, prow), prow), pl.ds(wide_l, thin_l)]

    def length(w, d):
        return STEPS if w == d else STEPS - 1

    def block(d, s):
        return lax.rem(z + (NZ - s if d == 0 else s), NZ)

    def z1(w, d, s):
        ref = wide(w, block(d, s))
        return remote(ref, ref, z1_ss.at[w, d, s], z1_rs.at[w, d, s], at(x, z + 1 if d == 0 else z - 1))

    def z2(w, d, s):
        ref = thin(w, x, block(d, s))
        return remote(ref, ref, z2_ss.at[w, d, s], z2_rs.at[w, d, s], at(x, z + 1 if d == 0 else z - 1))

    def slot_block(d, s, own_slot):
        return jnp.where(own_slot, z, block(d, s + 1)) if not isinstance(own_slot, bool) else (
            z if own_slot else block(d, s + 1)
        )

    def x2(w, e, d, s, own_slot=False):
        ref = thin(w, x, slot_block(d, s, own_slot))
        return remote(ref, ref, x2_ss.at[w, e], x2_rs.at[w, e, d, s], at(x + 1 - 2 * e, z))

    def xf(w, d, s, own_slot=False):
        ref = thin(w, lax.rem(x + (NX - 1 if d == 0 else 1), NX), slot_block(d, s, own_slot))
        return remote(ref, ref, xf_ss.at[w], xf_rs.at[w], at(x + 1 - 2 * d, z))

    def xd(w, d, s):
        ref = thin(w, x, block(d, s + 1))
        return remote(ref, ref, xf_ss.at[w], xf_rs.at[w], at(x + 2, z))

    def bulk(w, ss, rs):
        ref = wts.at[w, 0, :, pl.ds(wide_l, thin_l)]
        return remote(ref, ref, ss, rs, at(x + 1, z))

    for c in loads[:2]:
        c.wait()
    for a in range(7):
        kers[a, 0:7, :] = dker[a].astype(f32)
    low4 = lax.broadcasted_iota(jnp.int32, (8, chans), 0) < 4

    def pack(q, _):
        v = [feat[4 * q + i].astype(f32) for i in range(4)]
        turned = [pltpu.roll(t, 4, 0) for t in v]
        right = [jnp.where(low4, turned[i], v[i + 1]) for i in (0, 2)]
        left = [jnp.where(low4, v[i], turned[i + 1]) for i in (0, 2)]
        csend[0, q] = jnp.concatenate(right, 0).astype(bf16)
        csend[1, q] = jnp.concatenate(left, 0).astype(bf16)
        return 0

    lax.fori_loop(0, rows // 4, pack, 0)

    last = rows // 4 - 1

    def h_copy(side, c):
        src = csend.at[side, pl.ds(2 * c, 2)]
        dst = crecv.at[side, pl.ds(2 * c + 1, 2)]
        return remote(src, dst, hc_ss.at[side, c], hc_rs.at[side, c], (lat, (east, west)[side]))

    to_down = [
        remote(feat.at[pl.ds(rows - 3, 3)], rrecv.at[0], h_ss.at[0], h_rs.at[0], (lat + 1, lon)),
        remote(csend.at[0, last], crecv.at[0, 0], h_ss.at[1], h_rs.at[1], (lat + 1, east)),
        remote(csend.at[1, last], crecv.at[1, 0], h_ss.at[2], h_rs.at[2], (lat + 1, west)),
    ]
    to_up = [
        remote(feat.at[pl.ds(0, 3)], rrecv.at[1], h_ss.at[3], h_rs.at[3], (lat - 1, lon)),
        remote(csend.at[0, 0], crecv.at[0, last + 2], h_ss.at[4], h_rs.at[4], (lat - 1, east)),
        remote(csend.at[1, 0], crecv.at[1, last + 2], h_ss.at[5], h_rs.at[5], (lat - 1, west)),
    ]

    for c in own_copy:
        c.wait()
    for w in range(2):
        y_copy(w).wait_recv()
        for d in range(2):
            z2(w, d, 0).start()
        for e in range(2):
            x2(w, e, 1 - w, STEPS - 1, True).start()
    for c in range(2):
        for side in range(2):
            h_copy(side, c).start()

    @pl.when(has_down)
    def _():
        for c in to_down:
            c.start()

    @pl.when(has_up)
    def _():
        for c in to_up:
            c.start()

    def widen(h, _):
        v = feat[h].astype(f32)
        for t in range(tiles):
            xpad[t, h + 4, 8:16, :] = v[:, t * 128 : (t + 1) * 128]
        return 0

    lax.fori_loop(0, rows, widen, 0)

    def thin_step(w, s):
        for d in range(2):
            if isinstance(s, int) and s >= length(w, d):
                continue
            z2(w, d, s).wait_recv()
            if not isinstance(s, int) or s + 1 < length(w, d):
                z2(w, d, s + 1).start()
            for e in range(2):
                x2(w, e, d, s).start()
            if isinstance(s, int) and s >= DIRECT:
                xd(w, d, s).start()
        if isinstance(s, int) and s == 0:
            x2(w, 1 - w, 1 - w, STEPS - 1, True).wait_recv()
            xf(w, 1 - w, STEPS - 1, True).start()
        elif not isinstance(s, int) or s <= DIRECT:
            for d in range(2):
                cross_step(w, d, s - 1)

    def cross_step(w, d, s):
        x2(w, d, d, s).wait_recv()
        xf(w, d, s).start()

    def wide_step(w, s):
        for d in range(2):
            if isinstance(s, int) and s >= length(w, d):
                continue
            z1(w, d, s).wait_recv()
            if not isinstance(s, int) or s + 1 < length(w, d):
                z1(w, d, s + 1).start()

    def gathered(w):
        for d in range(2):

            def one(s, _, d=d):
                x2(w, 1 - d, d, s).wait_recv()
                return 0

            lax.fori_loop(0, STEPS, one, 0)
            for s in range(DIRECT, length(w, d)):
                x2(w, d, d, s).wait_recv()
        bulk(w, xf_ss.at[w], xf_rs.at[w]).wait_recv()

    for w in range(2):
        for k in range(1, NX):
            for i in range(2):
                x1(w, k, i).wait_recv()
        for d in range(2):
            z1(w, d, 0).start()
    for side in range(2):
        h_copy(side, 2).start()
    for s in range(EARLY + 1):
        for w in range(2):
            thin_step(w, s)
            if s > 0:
                wide_step(w, s - 1)
        if s == 0:
            for side in range(2):
                h_copy(side, 3).start()
    for c in loads[2:]:
        c.wait()

    def place(q):
        for side, lo in ((0, 4), (1, 16)):
            v = crecv[side, q].astype(f32)
            for i in range(4):
                for t in range(tiles):
                    xpad[t, 4 * q + i, lo : lo + 4, :] = v[4 * i : 4 * i + 4, t * 128 : (t + 1) * 128]

    def chunk_in(c):
        for side in range(2):
            h_copy(side, c).wait_recv()

        def one(i, _):
            place(2 * c + 1 + i)
            return 0

        lax.fori_loop(0, 2, one, 0)

    chunk_in(0)

    def margin(present, copies, row0, q, slot):
        @pl.when(present)
        def _():
            for c in copies:
                c.wait_recv()
            place(q)
            for r in range(3):
                v = rrecv[slot, r].astype(f32)
                for t in range(tiles):
                    xpad[t, row0 + r, 8:16, :] = v[:, t * 128 : (t + 1) * 128]

        @pl.when(jnp.logical_not(present))
        def _():
            for r in range(3):
                for t in range(tiles):
                    xpad[t, row0 + r] = jnp.zeros((24, 128), f32)

    margin(has_up, to_down, 1, 0, 0)

    def conv_tile(rb, t):
        lanes = pl.ds(pl.multiple_of(t * 128, 128), 128)
        acc = [jnp.broadcast_to(dbias[:, lanes], (8, 128)) for _ in range(8)]
        for b in range(7):
            win = [xpad[t, rb * 8 + 1 + r, 5 + b : 13 + b, :] for r in range(14)]
            for a in range(7):
                k = jnp.broadcast_to(kers[a, b : b + 1, lanes], (8, 128))
                for o in range(8):
                    acc[o] = acc[o] + win[o + a] * k
        for o in range(8):
            conv[pl.ds(pl.multiple_of((rb * 8 + o) * 8, 8), 8), lanes] = acc[o]

    def norm_group(rb, g):
        px = pl.ds(pl.multiple_of(rb * chunk + g * 16, 16), 16)
        v = conv[px, :]
        v = v - jnp.mean(v, axis=-1, keepdims=True)
        var = jnp.mean(v * v, axis=-1, keepdims=True)
        v = v * lax.rsqrt(var + 1e-06) * gain[...] + nbias[...]
        acts[lat, px, :] = v.astype(bf16)

    def act(slot, c):
        return acts.at[slot, pl.ds(pl.multiple_of(c * chunk, chunk), chunk), :]

    def a_sib(c):
        return remote(act(lat, c), act(lat, c), a_ss.at[0, c], a_rs.at[0, c], sib)

    def a_crs(c):
        return remote(act(lat, c), act(lat, c), a_ss.at[1, c], a_rs.at[1, c], crs)

    def a_fwd(c):
        return remote(act(far, c), act(far, c), a_ss.at[2, c], a_rs.at[2, c], sib)

    def conv_block(rb, _):
        @pl.when(rb < blocks - 1)
        def _():
            chunk_in(rb + 1)

        @pl.when(rb == blocks - 1)
        def _():
            margin(has_down, to_up, rows + 4, last + 2, 1)

        def run(t, _):
            conv_tile(rb, t)
            return 0

        lax.fori_loop(0, tiles // 2, run, 0)
        thin_step(0, rb + EARLY + 1)
        wide_step(0, rb + EARLY)
        lax.fori_loop(tiles // 2, tiles, run, 0)

        def run_norm(g, _):
            norm_group(rb, g)
            return 0

        lax.fori_loop(0, chunk // 16, run_norm, 0)
        a_crs(rb).start()
        a_sib(rb).start()
        thin_step(1, rb + EARLY + 1)
        wide_step(1, rb + EARLY)
        return 0

    lax.fori_loop(0, blocks, conv_block, 0)

    def forward(c):
        a_crs(c).wait_recv()
        a_fwd(c).start()

    pending = list(range(blocks))
    for s in range(EARLY + blocks, STEPS + 1):
        for w in range(2):
            if s + 1 < STEPS:
                thin_step(w, s + 1)
            if s < STEPS:
                wide_step(w, s)
            if w == 0 and pending:
                forward(pending.pop(0))
    for c in pending:
        forward(c)
    gathered(0)

    def pointwise(q, h):
        def one(n, _):
            lanes = pl.ds(pl.multiple_of(n * 256, 256), 256)
            wt = wts[0, :, :, lanes].reshape(chans, 256)
            pre = jnp.dot(acts[q], wt, preferred_element_type=f32) + ubias[:, lanes]
            act_ = 0.5 * pre * (1.0 + lax.erf(pre * 0.7071067811865476))
            hid[h, :, lanes] = act_.astype(bf16)
            return 0

        lax.fori_loop(0, hidden // 256, one, 0)

    def project(n, h):
        return lax.dot_general(hid[h], wts[1, n], (((1,), (1,)), ((), ())), preferred_element_type=f32)

    def o_copy(kind, n):
        src, dst, device = ((s_sib, r_sib, sib), (s_mid, r_mid, crs), (s_crs, r_crs, sib))[kind]
        return remote(src.at[n], dst.at[n], o_ss.at[kind, n], o_rs.at[kind, n], device)

    parts = NX
    for c in range(blocks):
        a_sib(c).wait_recv()
        a_fwd(c).wait_recv()

    pointwise(far_flip, 0)
    pointwise(far, 1)
    gathered(1)

    def first_part(n):
        s_sib[n] = project(n, 0).astype(bf16)
        o_copy(0, n).start()

    def second_part(n):
        total = project(n, 1)
        o_copy(0, n).wait_recv()
        s_mid[n] = (total + r_sib[n].astype(f32)).astype(bf16)
        o_copy(1, n).start()

    first_part(0)

    def both_parts(n, _):
        first_part(n + 1)
        second_part(n)
        return 0

    lax.fori_loop(0, parts - 1, both_parts, 0)
    second_part(parts - 1)

    pointwise(flip, 0)

    def third_part(n, _):
        s_crs[n] = project(n, 0).astype(bf16)
        o_copy(2, n).start()
        return 0

    lax.fori_loop(0, parts, third_part, 0)

    pointwise(lat, 1)

    def own_part(n, _):
        own[n] = project(n, 1)
        return 0

    lax.fori_loop(0, parts, own_part, 0)

    def finish(n, _):
        width = chans // parts
        lanes = pl.ds(pl.multiple_of(n * width, width), width)
        o_copy(2, n).wait_recv()
        part = own[n] + r_crs[n].astype(f32)
        o_copy(1, n).wait_recv()
        part = part + r_mid[n].astype(f32)
        part = scale[:, lanes] * (part + obias[:, lanes])
        res = feat[:, :, lanes].astype(f32) + part.reshape(rows, cols, width)
        out[:, :, lanes] = res.astype(bf16)
        return 0

    lax.fori_loop(0, parts, finish, 0)

    for w in range(2):
        y_copy(w).wait_send()
        for k in range(1, NX):
            for i in range(2):
                x1(w, k, i).wait_send()
        for e in range(2):
            bulk(w, x2_ss.at[w, e], xf_rs.at[w]).wait_send()
        bulk(w, xf_ss.at[w], xf_rs.at[w]).wait_send()
        for d in range(2):

            def gone(s, _, w=w, d=d):
                z1(w, d, s).wait_send()
                z2(w, d, s).wait_send()
                return 0

            lax.fori_loop(0, length(w, d), gone, 0)
    for side in range(2):
        for c in range(blocks):
            h_copy(side, c).wait_send()

    @pl.when(has_down)
    def _():
        for c in to_down:
            c.wait_send()

    @pl.when(has_up)
    def _():
        for c in to_up:
            c.wait_send()

    for c in range(blocks):
        a_sib(c).wait_send()
        a_crs(c).wait_send()
        a_fwd(c).wait_send()
    for n in range(parts):
        for kind in range(3):
            o_copy(kind, n).wait_send()


def local(
    features, depth_kernel, depth_bias, norm_gain, norm_bias, up_weight, up_bias, down_weight, down_bias, layer_scale
):
    rows, cols, chans = features.shape
    shard, hidden = up_weight.shape
    pixels = rows * cols
    bf16, f32 = jnp.bfloat16, jnp.float32
    vmem, dma = pltpu.VMEM, pltpu.SemaphoreType.DMA
    blocks = rows // 8
    flat = lambda v: v.reshape(1, -1)
    spec = pl.BlockSpec(memory_space=pltpu.VMEM)
    piece = (NX, pixels, chans // NX)
    return pl.pallas_call(
        kernel,
        out_shape=jax.ShapeDtypeStruct(features.shape, features.dtype),
        in_specs=[pl.BlockSpec(memory_space=pltpu.HBM)] * 10,
        out_specs=spec,
        scratch_shapes=[
            vmem(features.shape, bf16),
            vmem(depth_kernel.shape, bf16),
            vmem((1, chans), f32),
            vmem((1, chans), f32),
            vmem((1, chans), f32),
            vmem((1, hidden), f32),
            vmem((1, chans), f32),
            vmem((1, chans), f32),
            vmem((2, NX, chans // NX, hidden), bf16),
            vmem((chans // 128, rows + 8, 24, 128), f32),
            vmem((7, 8, chans), f32),
            vmem((pixels, chans), f32),
            vmem((2, rows // 4, 16, chans), bf16),
            vmem((2, rows // 4 + 2, 16, chans), bf16),
            vmem((2, 3, cols, chans), bf16),
            vmem((4, pixels, chans), bf16),
            vmem((2, pixels, hidden), bf16),
            vmem(piece, f32),
            vmem(piece, bf16),
            vmem(piece, bf16),
            vmem(piece, bf16),
            vmem(piece, bf16),
            vmem(piece, bf16),
            vmem(piece, bf16),
            dma((8,)), dma((2,)),
            dma((2,)), dma((2,)),
            dma((6,)), dma((6,)),
            dma((2, blocks)), dma((2, blocks)),
            dma((2, NX - 1, 2)), dma((2, NX - 1, 2)),
            dma((2, 2)), dma((2, 2, 2, STEPS)),
            dma((2,)), dma((2,)),
            dma((2, 2, STEPS)), dma((2, 2, STEPS)),
            dma((2, 2, STEPS)), dma((2, 2, STEPS)),
            dma((3, blocks)), dma((3, blocks)),
            dma((3, NX)), dma((3, NX)),
        ],
        compiler_params=pltpu.CompilerParams(
            collective_id=0, has_side_effects=True, vmem_limit_bytes=63 << 20
        ),
    )(
        features, depth_kernel, flat(depth_bias), flat(norm_gain), flat(norm_bias), up_weight, flat(up_bias),
        down_weight, flat(down_bias), flat(layer_scale),
    )


def solution(mesh):
    placed = (
        P("lat", "lon", None), P(), P(), P(), P(), P("lon", "lat"), P("lat"), P("lon", "lat"), P(), P(),
    )
    return jax.shard_map(
        local, mesh=mesh, in_specs=placed, out_specs=P("lat", "lon", None), check_vma=False
    )
```
